32 devices in a mesh: lon: 16 (over z, y, x), lev: 2 (over core).
Axes of the slice: x: 2, y: 2, z: 4, core: 2. Of those that a mesh axis runs over, the one named last changes fastest.
Arguments:
- ensemble: float32 [80, 16, 16384], P(None, 'lev', 'lon'), may hold values from -6 to 6
- obs_cell: int32 [12, 128], P(None, 'lon'), may hold values from 0 to 16383, as said below
- obs_value: float32 [12, 128], P(None, 'lon'), may hold values from -5 to 5
- obs_noise: float32 [12, 128], P(None, 'lon'), may hold values from 0.2 to 2
- obs_weight: float32 [12, 16, 128], P(None, 'lev'), may hold values from 0.05 to 0.5
- tile_lists: int32 [12, 384], P(None, 'lon'), may hold values from 0 to 128, as said below
- batch_order: int32 [12], replicated, may hold values from 0 to 11, each once
Outputs:
- analysis: float32 [80, 16, 16384], P(None, 'lev', 'lon')
The draws below stay inside these ranges and needn't reach their ends.
Inputs may be any that keep to these rules, and one draw needn't show every extreme that they name: `obs_cell`: each tile holds at most 8 observations of one block, and some tile exactly 8. `tile_lists`: for block b and tile t the tile's 24 slots hold first, ascending and once each, the observations of block b whose tile is t or a neighbour of t around the globe, then the value 128 in every remaining slot; in every block some tile has all 24 slots used. `batch_order`: each block once.
All inputs are finite; a program needn't handle non-finite values.
Results may differ from the reference program's by a relative error of at most 0.0003.
Values sent between devices are 32-bit elements; how exact they have to be, the bound alone decides.
A program may use at most 128 MiB of HBM per device.

```python
import math
import jax
import jax.numpy as jnp
from jax import lax

MEM = 80
OBS = 128
OWN_MAX = 8
ROUTE_CAP = 24
LON_DEV = 16
CELL_DEV = 1024
BATCHES = 12
LEVELS = 16
CELLS = 16384
N_LON = 16


def block_layout(key):
    subkeys = jax.random.split(jax.random.fold_in(key, 7351), BATCHES)

    def single(subkey):
        pick_key = jax.random.fold_in(subkey, 0)
        order_key = jax.random.fold_in(subkey, 1)
        cell_key = jax.random.fold_in(subkey, 2)
        shuffle_key = jax.random.fold_in(subkey, 4)
        slot_count = N_LON * OWN_MAX
        slot_tile = jnp.arange(slot_count, dtype=jnp.int32) // OWN_MAX
        centre = jax.random.randint(pick_key, (), 0, N_LON)
        forward = (slot_tile - centre) % N_LON
        backward = (centre - slot_tile) % N_LON
        nearby = (jnp.minimum(forward, backward) <= 1).astype(jnp.int32)
        score = jax.random.permutation(order_key, slot_count).astype(jnp.int32) + nearby * slot_count
        chosen = lax.top_k(score, OBS)[1].astype(jnp.int32)
        chosen = jax.random.permutation(shuffle_key, chosen)
        tiles = slot_tile[chosen]
        cell_ids = tiles * CELL_DEV + jax.random.randint(cell_key, (OBS,), 0, CELL_DEV)
        tile_ids = jnp.arange(N_LON, dtype=jnp.int32)
        distance_tiles = (tiles[None, :] - tile_ids[:, None]) % N_LON
        reached = (distance_tiles <= 1) | (distance_tiles == N_LON - 1)
        total = jnp.sum(reached.astype(jnp.int32), axis=1)
        numbers = jnp.arange(OBS, dtype=jnp.int32)
        ordering = jnp.where(reached, numbers[None, :], numbers[None, :] + OBS)
        ordered = jnp.argsort(ordering, axis=1, stable=True)[:, :ROUTE_CAP].astype(jnp.int32)
        slot_ids = jnp.arange(ROUTE_CAP, dtype=jnp.int32)
        lists = jnp.where(slot_ids[None, :] < total[:, None], ordered, OBS)
        return (cell_ids, lists.reshape(-1).astype(jnp.int32))
    return jax.vmap(single)(subkeys)


def draw_obs_cell(key, part):
    return block_layout(key)[0]


def draw_tile_lists(key, part):
    return block_layout(key)[1]


def shard_levels(stream_key, shape, cuts, least, top_value):
    gain, own = 1.0, jax.random.fold_in(stream_key, 6)
    for axis_at, parts in cuts:
        draws = jnp.exp(jax.random.uniform(jax.random.fold_in(own, axis_at), (parts,), jnp.float32, least / len(cuts), top_value / len(cuts)))
        gain = gain * jnp.repeat(draws, shape[axis_at] // parts).reshape([-1 if axis == axis_at else 1 for axis in range(len(shape))])
    return gain


def normal_values(key, extent, scale, limit, shards=(), held_as=jnp.bfloat16):
    entries = jax.random.normal(key, extent, jnp.float32) * scale
    if len(shards) > 0:
        entries = shard_levels(key, extent, shards, -0.22, 0.18) * entries
    return jnp.clip(entries, min=-limit, max=limit).astype(held_as)


def setup_inputs(seed: int = 0) -> dict:
    streams_of = jax.random.split(jax.random.key(seed), 8)
    return {
        "ensemble": normal_values(streams_of[0], (MEM, LEVELS, CELLS), 1.0, 6.0, ((1, 2), (2, 16)), jnp.float32),
        "obs_cell": draw_obs_cell(jax.random.fold_in(streams_of[7], 71), 0),
        "obs_value": normal_values(streams_of[2], (BATCHES, OBS), 1.0, 5.0, ((1, 16),), jnp.float32),
        "obs_noise": jnp.clip(jnp.exp(math.log(2.0) - 2.3025851 * jax.random.uniform(streams_of[3], (BATCHES, OBS), jnp.float32) ** shard_levels(streams_of[3], (BATCHES, OBS), ((1, 16),), -0.2, 0.2)), 0.2, 2.0),
        "obs_weight": jnp.clip(jnp.exp(math.log(0.5) - 2.3025851 * jax.random.uniform(streams_of[4], (BATCHES, LEVELS, OBS), jnp.float32) ** shard_levels(streams_of[4], (BATCHES, LEVELS, OBS), ((1, 2),), -0.2, 0.2)), 0.05, 0.5),
        "tile_lists": draw_tile_lists(jax.random.fold_in(streams_of[7], 71), 0),
        "batch_order": jax.random.permutation(streams_of[6], BATCHES).astype(jnp.int32),
    }


highest = lax.Precision.HIGHEST

def locate(cell_ids):
    within = cell_ids % CELL_DEV
    return (within // LON_DEV, cell_ids // CELL_DEV * LON_DEV + within % LON_DEV)

def taper_weight(source_ids, target_ids, circle):
    source_row, source_col = locate(source_ids)
    target_row, target_col = locate(target_ids)
    apart_cols = jnp.abs(source_col[:, None] - target_col[None, :])
    apart_cols = jnp.minimum(apart_cols, circle - apart_cols)
    apart_rows = source_row[:, None] - target_row[None, :]
    square = (apart_cols * apart_cols + apart_rows * apart_rows).astype(jnp.float32)
    return jnp.exp(square * (-2.0 / (LON_DEV * LON_DEV)))

def gain_parts(sample_now, observed, noise):
    centre = lax.optimization_barrier(jnp.mean(sample_now, axis=0))
    spread = sample_now - centre
    covariance = jnp.dot(spread.T, spread, precision=highest) / (MEM - 1) + jnp.diag(noise)
    factor = jnp.linalg.cholesky(covariance)
    innovation = (observed - centre)[:, None]
    halfway = lax.linalg.triangular_solve(factor, innovation, left_side=True, lower=True)
    kalman_gain = lax.linalg.triangular_solve(factor, halfway, left_side=True, lower=True, transpose_a=True)[:, 0]
    rooted = factor + jnp.diag(jnp.sqrt(noise))
    identity = jnp.eye(OBS, dtype=noise.dtype)
    within = lax.linalg.triangular_solve(rooted, identity, left_side=True, lower=True)
    reduced = lax.linalg.triangular_solve(factor, within, left_side=True, lower=True, transpose_a=True)
    return (spread, kalman_gain, reduced)

def update_block(block, spread, kalman_gain, reduced, chosen, usable, obs_ids, local_ids, circle):
    levels = block.shape[1]
    rows_used = chosen.shape[0]
    weight = taper_weight(obs_ids[chosen], local_ids, circle) * usable[:, None]
    centre = lax.optimization_barrier(jnp.mean(block, axis=0))
    flattened = (block - centre).reshape(MEM, -1)
    crossed = jnp.dot(spread[:, chosen].T, flattened, precision=highest) / (MEM - 1)
    tapered = (crossed.reshape(rows_used, levels, -1) * weight[:, None, :]).reshape(rows_used, -1)
    shifted = jnp.dot(kalman_gain[chosen], tapered, precision=highest)
    mixing = jnp.dot(spread, reduced[chosen].T, precision=highest)
    flattened = flattened - jnp.dot(mixing, tapered, precision=highest)
    return ((centre.reshape(-1) + shifted)[None, :] + flattened).reshape(block.shape)

def reference(ensemble, obs_cell, obs_value, obs_noise, obs_weight, tile_lists, batch_order):
    circle = LON_DEV * N_LON
    tiles = ensemble.reshape(MEM, LEVELS, N_LON, CELL_DEV).transpose(2, 0, 1, 3)
    tile_ids = jnp.arange(N_LON, dtype=jnp.int32)

    def serial(tiles, position):
        current = batch_order[position]
        cell_ids = obs_cell[current]
        owners = cell_ids // CELL_DEV
        within = cell_ids % CELL_DEV
        picked = tiles[owners, :, :, within]
        probe = lax.optimization_barrier(jnp.sum(picked * obs_weight[current].T[:, None, :], axis=2)).T
        spread, kalman_gain, reduced = gain_parts(probe, obs_value[current], obs_noise[current])
        lists = tile_lists[current].reshape(N_LON, ROUTE_CAP)
        filled = (lists < OBS).astype(jnp.float32)
        safe = jnp.minimum(lists, OBS - 1).astype(jnp.int32)

        def single(items):
            block, chosen, usable, tile_index = items
            local_ids = tile_index * CELL_DEV + jnp.arange(CELL_DEV, dtype=jnp.int32)
            return update_block(block, spread, kalman_gain, reduced, chosen, usable, cell_ids, local_ids, circle)
        tiles = lax.map(single, (tiles, safe, filled, tile_ids))
        return (tiles, None)
    tiles, unused = lax.scan(serial, tiles, jnp.arange(BATCHES, dtype=jnp.int32))
    return tiles.transpose(1, 2, 0, 3).reshape(MEM, LEVELS, CELLS)
```

```python
import functools

import jax
import jax.numpy as jnp
from jax import lax
from jax.experimental import pallas as pl
from jax.experimental.pallas import tpu as pltpu
from jax.sharding import PartitionSpec as P

LON_DEV = 16
CELL_DEV = 1024
PANEL = 8

highest = lax.Precision.HIGHEST
f32 = jnp.float32
bf16 = jnp.bfloat16


def split(x):
    high = x.astype(bf16)
    low = (x - high.astype(f32)).astype(bf16)
    return high, low


def dot(a, b):
    return jnp.dot(a, b, preferred_element_type=f32)


def tapered_weight(row_a, col_a, row_c, col_c, circle):
    e = jnp.abs(col_a - col_c)
    e = jnp.minimum(e, circle - e)
    d = row_a - row_c
    return jnp.exp((e * e + d * d) * (-2.0 / (LON_DEV * LON_DEV)))


def eliminate(a_ref, b_ref, noise_root, mem, obs, width):
    lane = lax.broadcasted_iota(jnp.int32, (1, obs), 1)
    sample = lax.broadcasted_iota(jnp.int32, (1, width), 1) < mem
    for start in range(0, obs, PANEL):
        spot = [[None] * PANEL for _ in range(PANEL)]
        for i in range(PANEL):
            for s in range(i + 1):
                spot[i][s] = jnp.broadcast_to(
                    a_ref[start + i : start + i + 1, start + s : start + s + 1], (1, obs)
                )
        in_panel = (lane >= start) & (lane < start + PANEL)
        rows = []
        sides = []
        for i in range(PANEL):
            row = a_ref[start + i : start + i + 1, :]
            rows.append(jnp.where(in_panel, jnp.where(lane == start + i, 1.0, 0.0), row))
            sides.append(b_ref[start + i : start + i + 1, :])
        scaled_rows = []
        scaled_sides = []
        for r in range(PANEL):
            pivot = spot[r][r]
            inverse_root = lax.rsqrt(pivot)
            inverse = inverse_root * inverse_root
            root = pivot * inverse_root
            added = jnp.where(sample, noise_root[start + r], 0.0)
            factor = 1.0 / (root + added)
            below = [spot[i][r] * inverse for i in range(r + 1, PANEL)]
            for n, i in enumerate(range(r + 1, PANEL)):
                for s in range(r + 1, i + 1):
                    spot[i][s] = spot[i][s] - below[n] * spot[s][r]
            solved = sides[r] * factor
            passing = solved * root
            for n, i in enumerate(range(r + 1, PANEL)):
                rows[i] = rows[i] - below[n] * rows[r]
                sides[i] = sides[i] - below[n] * passing
            scaled_rows.append(rows[r] * inverse)
            scaled_sides.append(solved * inverse_root)
            a_ref[start + r : start + r + 1, :] = jnp.where(
                lane < start + PANEL, rows[r] * inverse_root, 0.0
            )
            b_ref[start + r : start + r + 1, :] = solved
        after = start + PANEL
        if after < obs:
            upper = jnp.concatenate(rows, axis=0)
            left = upper.T[after:, :]
            right = jnp.concatenate(
                [jnp.concatenate(scaled_rows, axis=0), jnp.concatenate(scaled_sides, axis=0)], axis=1
            )
            change = jnp.dot(left, right, precision=highest, preferred_element_type=f32)
            a_ref[after:, :] = jnp.where(in_panel, 0.0, a_ref[after:, :]) - change[:, :obs]
            b_ref[after:, :] = b_ref[after:, :] - change[:, obs:]


def kernel_body(
    x_ref, probe_ref, value_ref, noise_ref, noise_col_ref, cell_row_ref, cell_col_ref, list_ref,
    out_ref, probes, a_ref, b_ref, *, batches, levels, mem, obs, cells, slots, axis_size,
):
    tile = lax.axis_index("lon")
    circle = float(LON_DEV * axis_size)
    scale = 1.0 / (mem - 1)
    probes[...] = probe_ref[...]
    cell = lax.broadcasted_iota(jnp.int32, (1, cells), 1)
    here_row = (cell // LON_DEV).astype(f32)
    here_col = (tile * LON_DEV + cell % LON_DEV).astype(f32)
    target = cell_row_ref[...]
    target_tile = target // CELL_DEV
    target_within = target - target_tile * CELL_DEV
    target_row_int = target_within // LON_DEV
    target_col = (target_tile * LON_DEV + target_within - target_row_int * LON_DEV).astype(f32)
    target_row = target_row_int.astype(f32)
    target_tile = target_tile.astype(f32)
    lanes = lax.broadcasted_iota(jnp.int32, (obs, obs), 1)
    subs = lax.broadcasted_iota(jnp.int32, (obs, obs), 0)

    def turn(k, carry):
        now = probes[k]
        centre = jnp.mean(now, axis=0, keepdims=True)
        spread = now - centre
        innovation = value_ref[k] - centre
        padded = jnp.concatenate(
            [spread, innovation, jnp.zeros((obs - mem - 1, obs), f32)], axis=0
        )
        sides = padded.T
        noise_row = noise_ref[k]
        covariance = jnp.dot(sides[:, :mem], spread, precision=highest, preferred_element_type=f32) * scale
        a_ref[...] = covariance + jnp.where(lanes == subs, noise_row, 0.0)
        b_ref[...] = sides
        root_col = jnp.sqrt(noise_col_ref[k])
        roots = [root_col[j : j + 1, :] for j in range(obs)]
        eliminate(a_ref, b_ref, roots, mem, obs, obs)
        joined = lax.dot_general(
            a_ref[...], b_ref[...], (((0,), (0,)), ((), ())), precision=highest, preferred_element_type=f32
        )
        gain_t = joined[:, mem : mem + 1] - joined
        gain = gain_t.T[:mem, :]

        s_high, s_low = split(spread)
        stacked = jnp.concatenate([s_high.astype(f32), s_high.astype(f32), s_low.astype(f32)], axis=0)
        left = stacked.T.astype(bf16)
        g_high, g_low = split(gain)
        gains = jnp.concatenate([g_high, g_high, g_low], axis=1)

        cell_col = cell_col_ref[k]
        from_tile = cell_col // CELL_DEV
        from_within = cell_col - from_tile * CELL_DEV
        from_row = from_within // LON_DEV
        from_col = (from_tile * LON_DEV + from_within - from_row * LON_DEV).astype(f32)
        from_row = from_row.astype(f32)
        from_tile = from_tile.astype(f32)

        def renew(b, carry):
            @pl.when(2 * b + 1 > k)
            def _():
                upcoming = jnp.concatenate([probes[2 * b], probes[2 * b + 1]], axis=1)
                high, low = split(upcoming)
                crossed = dot(left, jnp.concatenate([high, low, high], axis=0))
                weights = []
                for u in range(2):
                    weight = tapered_weight(
                        from_row, from_col, target_row_ref_get(b, u), target_col_ref_get(b, u), circle
                    )
                    apart = jnp.abs(from_tile - target_tile_ref_get(b, u))
                    near = (apart < 1.5) | (apart > axis_size - 1.5)
                    weights.append(jnp.where(near, weight * scale, 0.0))
                tapered = crossed * jnp.concatenate(weights, axis=1)
                high, low = split(tapered)
                upcoming = upcoming + dot(gains, jnp.concatenate([high, low, high], axis=0))
                probes[2 * b] = upcoming[:, :obs]
                probes[2 * b + 1] = upcoming[:, obs:]

            return carry

        def target_row_ref_get(b, u):
            return target_row[2 * b + u]

        def target_col_ref_get(b, u):
            return target_col[2 * b + u]

        def target_tile_ref_get(b, u):
            return target_tile[2 * b + u]

        for b in range(batches // 2):
            renew(b, 0)

        listed = list_ref[k]
        chosen = lanes[:slots] == listed
        select = chosen.astype(bf16)
        pick_row = cell_row_ref[k]
        pick_tile = pick_row // CELL_DEV
        pick_within = pick_row - pick_tile * CELL_DEV
        pick_r = pick_within // LON_DEV
        pick_c = (pick_tile * LON_DEV + pick_within - pick_r * LON_DEV).astype(f32)
        list_row = jnp.sum(jnp.where(chosen, pick_r.astype(f32), 0.0), axis=1, keepdims=True)
        list_col = jnp.sum(jnp.where(chosen, pick_c, 0.0), axis=1, keepdims=True)
        usable = jnp.where(listed < obs, scale, 0.0)
        weight = tapered_weight(list_row, list_col, here_row, here_col, circle) * usable
        left_listed = dot(select, left).astype(bf16)
        gt_high, gt_low = split(gain_t)
        gt_high = dot(select, gt_high)
        gt_low = dot(select, gt_low)
        gains_listed = jnp.concatenate([gt_high, gt_high, gt_low, jnp.zeros((obs - 3 * slots, obs), f32)], axis=0)
        gains_listed = gains_listed.T[:mem, : 3 * slots].astype(bf16)

        def spread_level(level, carry, source):
            block = source[level]
            high, low = split(block)
            crossed = dot(left_listed, jnp.concatenate([high, low, high], axis=0))
            high, low = split(crossed * weight)
            out_ref[level] = block + dot(gains_listed, jnp.concatenate([high, low, high], axis=0))
            return carry

        lax.fori_loop(0, levels, functools.partial(spread_level, source=out_ref), 0)
        return carry

    out_ref[...] = x_ref[...]
    lax.fori_loop(0, batches, turn, 0)


def body(ensemble, obs_cell, obs_value, obs_noise, obs_weight, tile_lists, batch_order):
    mem, levels, cells = ensemble.shape
    batches = obs_cell.shape[0]
    axis_size = lax.axis_size("lon")
    obs = obs_cell.shape[1] * axis_size
    slots = 32
    cell_table = lax.all_gather(obs_cell, "lon", axis=1, tiled=True)
    observed = lax.all_gather(obs_value, "lon", axis=1, tiled=True)
    noise = lax.all_gather(obs_noise, "lon", axis=1, tiled=True)
    offset = lax.axis_index("lon") * CELL_DEV

    cell_table = cell_table[batch_order]
    observed = observed[batch_order]
    noise = noise[batch_order]
    weights = obs_weight[batch_order]
    lists = tile_lists[batch_order]

    owned = ((cell_table >= offset) & (cell_table < offset + CELL_DEV)).astype(f32)
    within = jnp.clip(cell_table - offset, 0, CELL_DEV - 1)

    def portion_of(inside, mine, weight):
        picked = jnp.take(ensemble, inside, axis=2)
        return jnp.sum(picked * (weight * mine[None, :])[None], axis=1)

    probes = lax.psum(jax.vmap(portion_of)(within, owned, weights), ("lon", "lev"))
    lists = jnp.pad(lists, ((0, 0), (0, slots - lists.shape[1])), constant_values=obs)

    call = pl.pallas_call(
        functools.partial(
            kernel_body, batches=batches, levels=levels, mem=mem, obs=obs, cells=cells, slots=slots,
            axis_size=axis_size,
        ),
        out_shape=jax.ShapeDtypeStruct((levels, mem, cells), f32),
        in_specs=[pl.BlockSpec(memory_space=pltpu.VMEM)] * 8,
        out_specs=pl.BlockSpec(memory_space=pltpu.VMEM),
        scratch_shapes=[
            pltpu.VMEM((batches, mem, obs), f32),
            pltpu.VMEM((obs, obs), f32),
            pltpu.VMEM((obs, obs), f32),
        ],
        compiler_params=pltpu.CompilerParams(vmem_limit_bytes=40 * 1024 * 1024),
        name="assimilate",
    )
    out = call(
        ensemble.transpose(1, 0, 2),
        probes,
        observed[:, None, :],
        noise[:, None, :],
        noise[:, :, None],
        cell_table[:, None, :],
        cell_table[:, :, None],
        lists[:, :, None],
    )
    return out.transpose(1, 0, 2)


def solution(mesh):
    return jax.shard_map(
        body,
        mesh=mesh,
        in_specs=(
            P(None, "lev", "lon"),
            P(None, "lon"),
            P(None, "lon"),
            P(None, "lon"),
            P(None, "lev", None),
            P(None, "lon"),
            P(),
        ),
        out_specs=P(None, "lev", "lon"),
        check_vma=False,
    )
```

```python
import functools

import jax
import jax.numpy as jnp
from jax import lax
from jax.experimental import pallas as pl
from jax.experimental.pallas import tpu as pltpu
from jax.sharding import PartitionSpec as P

LON_DEV = 16
CELL_DEV = 1024
PANEL = 8

highest = lax.Precision.HIGHEST
f32 = jnp.float32
bf16 = jnp.bfloat16


def split(x):
    high = x.astype(bf16)
    low = (x - high.astype(f32)).astype(bf16)
    return high, low


def dot(a, b):
    return jnp.dot(a, b, preferred_element_type=f32)


def tapered_weight(row_a, col_a, row_c, col_c, circle):
    e = jnp.abs(col_a - col_c)
    e = jnp.minimum(e, circle - e)
    d = row_a - row_c
    return jnp.exp((e * e + d * d) * (-2.0 / (LON_DEV * LON_DEV)))


def eliminate(a_ref, b_ref, noise_root, mem, obs, width):
    lane = lax.broadcasted_iota(jnp.int32, (1, obs), 1)
    sample = lax.broadcasted_iota(jnp.int32, (1, width), 1) < mem
    for start in range(0, obs, PANEL):
        spot = [[None] * PANEL for _ in range(PANEL)]
        for i in range(PANEL):
            for s in range(i + 1):
                spot[i][s] = jnp.broadcast_to(
                    a_ref[start + i : start + i + 1, start + s : start + s + 1], (1, obs)
                )
        in_panel = (lane >= start) & (lane < start + PANEL)
        rows = []
        sides = []
        for i in range(PANEL):
            row = a_ref[start + i : start + i + 1, :]
            rows.append(jnp.where(in_panel, jnp.where(lane == start + i, 1.0, 0.0), row))
            sides.append(b_ref[start + i : start + i + 1, :])
        scaled_rows = []
        scaled_sides = []
        for r in range(PANEL):
            pivot = spot[r][r]
            inverse_root = lax.rsqrt(pivot)
            inverse = inverse_root * inverse_root
            root = pivot * inverse_root
            added = jnp.where(sample, noise_root[start + r], 0.0)
            factor = 1.0 / (root + added)
            below = [spot[i][r] * inverse for i in range(r + 1, PANEL)]
            for n, i in enumerate(range(r + 1, PANEL)):
                for s in range(r + 1, i + 1):
                    spot[i][s] = spot[i][s] - below[n] * spot[s][r]
            solved = sides[r] * factor
            passing = solved * root
            for n, i in enumerate(range(r + 1, PANEL)):
                rows[i] = rows[i] - below[n] * rows[r]
                sides[i] = sides[i] - below[n] * passing
            scaled_rows.append(rows[r] * inverse)
            scaled_sides.append(solved * inverse_root)
            a_ref[start + r : start + r + 1, :] = jnp.where(
                lane < start + PANEL, rows[r] * inverse_root, 0.0
            )
            b_ref[start + r : start + r + 1, :] = solved
        after = start + PANEL
        if after < obs:
            upper = jnp.concatenate(rows, axis=0)
            left = upper.T[after:, :]
            right = jnp.concatenate(
                [jnp.concatenate(scaled_rows, axis=0), jnp.concatenate(scaled_sides, axis=0)], axis=1
            )
            change = jnp.dot(left, right, precision=highest, preferred_element_type=f32)
            a_ref[after:, :] = jnp.where(in_panel, 0.0, a_ref[after:, :]) - change[:, :obs]
            b_ref[after:, :] = b_ref[after:, :] - change[:, obs:]


def kernel_body(
    x_ref, probe_ref, value_ref, noise_ref, noise_col_ref, cell_row_ref, cell_col_ref, list_ref,
    out_ref, probes, a_ref, b_ref, *, batches, levels, mem, obs, cells, slots, axis_size,
):
    tile = lax.axis_index("lon")
    circle = float(LON_DEV * axis_size)
    scale = 1.0 / (mem - 1)
    probes[...] = probe_ref[...]
    cell = lax.broadcasted_iota(jnp.int32, (1, cells), 1)
    here_row = (cell // LON_DEV).astype(f32)
    here_col = (tile * LON_DEV + cell % LON_DEV).astype(f32)
    target = cell_row_ref[...]
    target_tile = target // CELL_DEV
    target_within = target - target_tile * CELL_DEV
    target_row_int = target_within // LON_DEV
    target_col = (target_tile * LON_DEV + target_within - target_row_int * LON_DEV).astype(f32)
    target_row = target_row_int.astype(f32)
    target_tile = target_tile.astype(f32)
    lanes = lax.broadcasted_iota(jnp.int32, (obs, obs), 1)
    subs = lax.broadcasted_iota(jnp.int32, (obs, obs), 0)

    def turn(k, carry):
        now = probes[k]
        centre = jnp.mean(now, axis=0, keepdims=True)
        spread = now - centre
        innovation = value_ref[k] - centre
        padded = jnp.concatenate(
            [spread, innovation, jnp.zeros((obs - mem - 1, obs), f32)], axis=0
        )
        sides = padded.T
        noise_row = noise_ref[k]
        covariance = jnp.dot(sides[:, :mem], spread, precision=highest, preferred_element_type=f32) * scale
        a_ref[...] = covariance + jnp.where(lanes == subs, noise_row, 0.0)
        b_ref[...] = sides
        root_col = jnp.sqrt(noise_col_ref[k])
        roots = [root_col[j : j + 1, :] for j in range(obs)]
        eliminate(a_ref, b_ref, roots, mem, obs, obs)
        joined = lax.dot_general(
            a_ref[...], b_ref[...], (((0,), (0,)), ((), ())), precision=highest, preferred_element_type=f32
        )
        gain_t = joined[:, mem : mem + 1] - joined
        gain = gain_t.T[:mem, :]

        s_high, s_low = split(spread)
        stacked = jnp.concatenate([s_high.astype(f32), s_high.astype(f32), s_low.astype(f32)], axis=0)
        left = stacked.T.astype(bf16)
        g_high, g_low = split(gain)
        gains = jnp.concatenate([g_high, g_high, g_low], axis=1)

        cell_col = cell_col_ref[k]
        from_tile = cell_col // CELL_DEV
        from_within = cell_col - from_tile * CELL_DEV
        from_row = from_within // LON_DEV
        from_col = (from_tile * LON_DEV + from_within - from_row * LON_DEV).astype(f32)
        from_row = from_row.astype(f32)
        from_tile = from_tile.astype(f32)

        def renew(b, carry):
            @pl.when(2 * b + 1 > k)
            def _():
                upcoming = jnp.concatenate([probes[2 * b], probes[2 * b + 1]], axis=1)
                high, low = split(upcoming)
                crossed = dot(left, jnp.concatenate([high, low, high], axis=0))
                weights = []
                for u in range(2):
                    weight = tapered_weight(
                        from_row, from_col, target_row_ref_get(b, u), target_col_ref_get(b, u), circle
                    )
                    apart = jnp.abs(from_tile - target_tile_ref_get(b, u))
                    near = (apart < 1.5) | (apart > axis_size - 1.5)
                    weights.append(jnp.where(near, weight * scale, 0.0))
                tapered = crossed * jnp.concatenate(weights, axis=1)
                high, low = split(tapered)
                upcoming = upcoming + dot(gains, jnp.concatenate([high, low, high], axis=0))
                probes[2 * b] = upcoming[:, :obs]
                probes[2 * b + 1] = upcoming[:, obs:]

            return carry

        def target_row_ref_get(b, u):
            return target_row[2 * b + u]

        def target_col_ref_get(b, u):
            return target_col[2 * b + u]

        def target_tile_ref_get(b, u):
            return target_tile[2 * b + u]

        for b in range(batches // 2):
            renew(b, 0)

        listed = list_ref[k]
        chosen = lanes[:slots] == listed
        select = chosen.astype(bf16)
        pick_row = cell_row_ref[k]
        pick_tile = pick_row // CELL_DEV
        pick_within = pick_row - pick_tile * CELL_DEV
        pick_r = pick_within // LON_DEV
        pick_c = (pick_tile * LON_DEV + pick_within - pick_r * LON_DEV).astype(f32)
        list_row = jnp.sum(jnp.where(chosen, pick_r.astype(f32), 0.0), axis=1, keepdims=True)
        list_col = jnp.sum(jnp.where(chosen, pick_c, 0.0), axis=1, keepdims=True)
        usable = jnp.where(listed < obs, scale, 0.0)
        weight = tapered_weight(list_row, list_col, here_row, here_col, circle) * usable
        left_listed = dot(select, left).astype(bf16)
        gt_high, gt_low = split(gain_t)
        gt_high = dot(select, gt_high)
        gt_low = dot(select, gt_low)
        gains_listed = jnp.concatenate([gt_high, gt_high, gt_low, jnp.zeros((obs - 3 * slots, obs), f32)], axis=0)
        gains_listed = gains_listed.T[:mem, : 3 * slots].astype(bf16)

        def spread_level(level, carry, source):
            block = source[level]
            high, low = split(block)
            crossed = dot(left_listed, jnp.concatenate([high, low, high], axis=0))
            high, low = split(crossed * weight)
            out_ref[level] = block + dot(gains_listed, jnp.concatenate([high, low, high], axis=0))
            return carry

        lax.fori_loop(0, levels, functools.partial(spread_level, source=out_ref), 0)
        return carry

    out_ref[...] = x_ref[...]
    lax.fori_loop(0, batches, turn, 0)


def peer_of(d, ranks, both):
    lon, lev = lax.axis_index("lon"), lax.axis_index("lev")
    if not both:
        return lax.rem(lon + d, ranks), lev
    cores = lax.axis_size("lev")
    number = lax.rem(lon * cores + lev + d, ranks)
    return lax.div(number, cores), lax.rem(number, cores)


def meet(ranks, both):
    barrier = pltpu.get_barrier_semaphore()

    def announce(d, carry):
        pl.semaphore_signal(
            barrier, inc=1, device_id=peer_of(d, ranks, both), device_id_type=pl.DeviceIdType.MESH
        )
        return carry

    lax.fori_loop(1, ranks, announce, 0)
    pl.semaphore_wait(barrier, ranks - 1)


def each_peer(ranks, copy_to):
    def start(d, carry):
        copy_to(d).start()
        return carry

    def finish(d, carry):
        copy_to(d).wait()
        return carry

    return (
        lambda: lax.fori_loop(1, ranks, start, 0),
        lambda: lax.fori_loop(1, ranks, finish, 0),
    )


def table_kernel(mine_ref, out_ref, landed, send_sem, recv_sem, *, ranks):
    meet(ranks, False)

    def copy_to(d):
        return pltpu.make_async_remote_copy(
            src_ref=mine_ref,
            dst_ref=landed.at[d],
            send_sem=send_sem.at[d],
            recv_sem=recv_sem.at[d],
            device_id=peer_of(d, ranks, False),
            device_id_type=pl.DeviceIdType.MESH,
        )

    start, finish = each_peer(ranks, copy_to)
    start()
    landed[0] = mine_ref[...]
    finish()
    out_ref[...] = jnp.sum(landed[...], axis=0)


def sum_kernel(mine_ref, out_ref, landed, total, send_sem, recv_sem, send_again, recv_again, *, ranks, rows):
    meet(ranks, True)
    me = lax.axis_index("lon") * lax.axis_size("lev") + lax.axis_index("lev")
    own = pl.ds(pl.multiple_of(me * rows, rows), rows)

    def scatter_to(d):
        other = lax.rem(me + d, ranks)
        return pltpu.make_async_remote_copy(
            src_ref=mine_ref.at[pl.ds(pl.multiple_of(other * rows, rows), rows)],
            dst_ref=landed.at[d],
            send_sem=send_sem.at[d],
            recv_sem=recv_sem.at[d],
            device_id=peer_of(d, ranks, True),
            device_id_type=pl.DeviceIdType.MESH,
        )

    def gather_to(d):
        return pltpu.make_async_remote_copy(
            src_ref=total,
            dst_ref=out_ref.at[own],
            send_sem=send_again.at[d],
            recv_sem=recv_again.at[d],
            device_id=peer_of(d, ranks, True),
            device_id_type=pl.DeviceIdType.MESH,
        )

    start, finish = each_peer(ranks, scatter_to)
    start()
    landed[0] = mine_ref[own]
    finish()
    total[...] = jnp.sum(landed[...], axis=0)
    start, finish = each_peer(ranks, gather_to)
    start()
    out_ref[own] = total[...]
    finish()


def gathered_table(parts, axis_size):
    rows, own = parts.shape
    padded = -(-rows // 8) * 8
    width = own * axis_size
    lane = jnp.arange(width, dtype=jnp.int32)[None, :]
    placed = jnp.where(lane // own == lax.axis_index("lon"), jnp.tile(parts, (1, axis_size)), 0.0)
    placed = jnp.pad(placed, ((0, padded - rows), (0, 0)))
    return pl.pallas_call(
        functools.partial(table_kernel, ranks=axis_size),
        out_shape=jax.ShapeDtypeStruct((padded, width), f32),
        in_specs=[pl.BlockSpec(memory_space=pltpu.VMEM)],
        out_specs=pl.BlockSpec(memory_space=pltpu.VMEM),
        scratch_shapes=[
            pltpu.VMEM((axis_size, padded, width), f32),
            pltpu.SemaphoreType.DMA((axis_size,)),
            pltpu.SemaphoreType.DMA((axis_size,)),
        ],
        compiler_params=pltpu.CompilerParams(collective_id=0, has_side_effects=True),
        name="table",
    )(placed)[:rows]


def summed(portions, ranks):
    count, width = portions.shape
    rows = -(-count // (8 * ranks)) * 8
    padded = jnp.pad(portions, ((0, rows * ranks - count), (0, 0)))
    return pl.pallas_call(
        functools.partial(sum_kernel, ranks=ranks, rows=rows),
        out_shape=jax.ShapeDtypeStruct(padded.shape, f32),
        in_specs=[pl.BlockSpec(memory_space=pltpu.VMEM)],
        out_specs=pl.BlockSpec(memory_space=pltpu.VMEM),
        scratch_shapes=[
            pltpu.VMEM((ranks, rows, width), f32),
            pltpu.VMEM((rows, width), f32),
            pltpu.SemaphoreType.DMA((ranks,)),
            pltpu.SemaphoreType.DMA((ranks,)),
            pltpu.SemaphoreType.DMA((ranks,)),
            pltpu.SemaphoreType.DMA((ranks,)),
        ],
        compiler_params=pltpu.CompilerParams(collective_id=1, has_side_effects=True),
        name="total",
    )(padded)[:count]


def body(ensemble, obs_cell, obs_value, obs_noise, obs_weight, tile_lists, batch_order):
    mem, levels, cells = ensemble.shape
    batches = obs_cell.shape[0]
    axis_size = lax.axis_size("lon")
    obs = obs_cell.shape[1] * axis_size
    slots = 32
    parts = jnp.concatenate([obs_cell.astype(f32), obs_value, obs_noise], axis=0)
    table = gathered_table(parts, axis_size)
    cell_table = table[:batches].astype(jnp.int32)
    observed = table[batches : 2 * batches]
    noise = table[2 * batches :]
    offset = lax.axis_index("lon") * CELL_DEV

    cell_table = cell_table[batch_order]
    observed = observed[batch_order]
    noise = noise[batch_order]
    weights = obs_weight[batch_order]
    lists = tile_lists[batch_order]

    owned = ((cell_table >= offset) & (cell_table < offset + CELL_DEV)).astype(f32)
    within = jnp.clip(cell_table - offset, 0, CELL_DEV - 1)

    def portion_of(inside, mine, weight):
        picked = jnp.take(ensemble, inside, axis=2)
        return jnp.sum(picked * (weight * mine[None, :])[None], axis=1)

    portions = jax.vmap(portion_of)(within, owned, weights).reshape(batches * mem, obs)
    probes = summed(portions, axis_size * lax.axis_size("lev")).reshape(batches, mem, obs)
    lists = jnp.pad(lists, ((0, 0), (0, slots - lists.shape[1])), constant_values=obs)

    call = pl.pallas_call(
        functools.partial(
            kernel_body, batches=batches, levels=levels, mem=mem, obs=obs, cells=cells, slots=slots,
            axis_size=axis_size,
        ),
        out_shape=jax.ShapeDtypeStruct((levels, mem, cells), f32),
        in_specs=[pl.BlockSpec(memory_space=pltpu.VMEM)] * 8,
        out_specs=pl.BlockSpec(memory_space=pltpu.VMEM),
        scratch_shapes=[
            pltpu.VMEM((batches, mem, obs), f32),
            pltpu.VMEM((obs, obs), f32),
            pltpu.VMEM((obs, obs), f32),
        ],
        compiler_params=pltpu.CompilerParams(vmem_limit_bytes=40 * 1024 * 1024),
        name="assimilate",
    )
    out = call(
        ensemble.transpose(1, 0, 2),
        probes,
        observed[:, None, :],
        noise[:, None, :],
        noise[:, :, None],
        cell_table[:, None, :],
        cell_table[:, :, None],
        lists[:, :, None],
    )
    return out.transpose(1, 0, 2)


def solution(mesh):
    return jax.shard_map(
        body,
        mesh=mesh,
        in_specs=(
            P(None, "lev", "lon"),
            P(None, "lon"),
            P(None, "lon"),
            P(None, "lon"),
            P(None, "lev", None),
            P(None, "lon"),
            P(),
        ),
        out_specs=P(None, "lev", "lon"),
        check_vma=False,
    )
```
